32 devices in a mesh: mode: 2 (over x), atom: 16 (over z, y, core).
Axes of the slice: x: 2, y: 2, z: 4, core: 2. Of those that a mesh axis runs over, the one named last changes fastest.
Arguments:
- velocities: bfloat16 [2, 16640, 384], P(None, 'atom'), may hold values from -6 to 6
- flux: bfloat16 [2, 16640, 384], P(None, 'atom'), may hold values from -6 to 6
- atom_ids: int32 [2, 16640], P(None, 'atom'), may hold values from 0 to 16383, as said below
- row_counts: int32 [2, 16], P(None, 'atom'), may hold values from 1008 to 1040, as said below
- vectors: bfloat16 [3, 16384, 1024], P(None, 'atom', 'mode'), may hold values from -0.0390625 to 0.0390625
Outputs:
- correlations: bfloat16 [16, 1024, 1024], P(None, ('mode', 'atom'))
The draws below stay inside these ranges and needn't reach their ends.
Inputs may be any that keep to these rules, and one draw needn't show every extreme that they name: `atom_ids`: in each frame block the used rows of all domains name every atom 0 to 16383 exactly once; unused rows hold arbitrary atom numbers. One domain holds at most 65 atoms of any one owner block a // 1024, and in every frame block some domain holds exactly 65 atoms of every owner block. `row_counts`: in every frame block the counts sum to 16384 and some domain uses all 1040 rows.
All inputs are finite; a program needn't handle non-finite values.
Results may differ from the reference program's by a relative error of at most 0.0057.
Values may be sent and summed in bfloat16 or wider, within the bound.
No kernel may reach another device: no remote copies, remote signals or barrier semaphores. Data moves between devices by JAX's collectives and lax.ppermute only.
A program may use at most 64 MiB of HBM per device.

```python
import jax
import jax.numpy as jnp
from jax import lax

MODE_DEV = 512
MODES = 1024
ATOM_DEV = 1024
ATOMS = 16384
DOM_ROWS = 1040
CAP = 65
FB_LEN = 128
FBLK = 2
FRAMES = 256
LAGS = 16
ANCHORS = 241
N_ATOM = 16


def routing_tables(key):
    base_key = jax.random.fold_in(key, 7701)

    def one_block(block_key):
        key_delta, key_forced, key_ranks, key_perm, key_shuffle, key_filler = jax.random.split(block_key, 6)
        pair_count = N_ATOM // 2
        shifts = jax.random.randint(key_delta, (pair_count,), -N_ATOM, N_ATOM + 1)
        forced = jax.random.randint(key_forced, (), 0, pair_count)
        shifts = jnp.where(jnp.arange(pair_count) == forced, N_ATOM, shifts)
        totals = ATOM_DEV + shifts
        base_count = totals // N_ATOM
        extra_count = totals % N_ATOM
        owner_ranks = jax.vmap(lambda sub_key: jax.random.permutation(sub_key, N_ATOM))(jax.random.split(key_ranks, pair_count))
        even_counts = base_count[:, None] + (owner_ranks < extra_count[:, None]).astype(jnp.int32)
        odd_counts = 2 * (ATOM_DEV // N_ATOM) - even_counts
        counts = jnp.stack([even_counts, odd_counts], axis=1).reshape(N_ATOM, N_ATOM)
        starts = jnp.cumsum(counts, axis=0) - counts
        owner_perm = jax.vmap(lambda sub_key: jax.random.permutation(sub_key, ATOM_DEV))(jax.random.split(key_perm, N_ATOM))
        slot_index = jnp.arange(CAP)
        position = jnp.minimum(starts[:, :, None] + slot_index[None, None, :], ATOM_DEV - 1)
        valid_slots = slot_index[None, None, :] < counts[:, :, None]
        owner_index = jnp.arange(N_ATOM)[None, :, None]
        local_ids = owner_perm[owner_index, position]
        grid_ids = (owner_index * ATOM_DEV + local_ids).reshape(N_ATOM, N_ATOM * CAP)
        flat_valid = valid_slots.reshape(N_ATOM, N_ATOM * CAP)
        shuffle = jax.vmap(lambda sub_key: jax.random.permutation(sub_key, DOM_ROWS))(jax.random.split(key_shuffle, N_ATOM))
        sort_score = jnp.where(flat_valid, 0, DOM_ROWS) + shuffle
        row_order = jnp.argsort(sort_score, axis=1)
        sorted_ids = jnp.take_along_axis(grid_ids, row_order, axis=1)
        row_totals = jnp.sum(flat_valid.astype(jnp.int32), axis=1)
        filler = jax.random.randint(key_filler, (N_ATOM, DOM_ROWS), 0, ATOMS)
        row_position = jnp.arange(DOM_ROWS)
        final_ids = jnp.where(row_position[None, :] < row_totals[:, None], sorted_ids, filler)
        return (final_ids.reshape(-1), row_totals)
    all_ids, all_counts = jax.vmap(one_block)(jax.random.split(base_key, FBLK))
    return (all_ids.astype(jnp.int32), all_counts.astype(jnp.int32))


def draw_atom_ids(key, part):
    return routing_tables(key)[0]


def draw_row_counts(key, part):
    return routing_tables(key)[1]


def strengthened(result, key, source, target, parts, factor):
    owner, partner = [(jnp.arange(result.shape[axis_at]) // (result.shape[axis_at] // parts)).reshape([-1 if axis == axis_at else 1 for axis in range(result.ndim)]) for axis_at in (source, target)]
    chosen = jax.random.permutation(key, parts)[partner]
    strong = (owner == chosen) | (owner == (partner + parts // 2) % parts)
    return jnp.where(strong, factor * result, result)


def level_of(key, extent, shards, smallest, largest):
    loudness = 1.0
    for axis_at, shards_of in shards:
        draws = jax.random.uniform(jax.random.fold_in(jax.random.fold_in(key, 6), axis_at), (shards_of,), jnp.float32, smallest / len(shards), largest / len(shards))
        loudness = loudness * jnp.repeat(jnp.exp(draws), extent[axis_at] // shards_of).reshape((-1,) + (1,) * (len(extent) - 1 - axis_at))
    return loudness


def gaussian(key, extent, width, reach, shards=(), held_as=jnp.bfloat16):
    array = width * jax.random.normal(key, extent, jnp.float32)
    if shards:
        array = array * level_of(key, extent, shards, -0.22, 0.18)
    return jnp.clip(array, -reach, reach).astype(held_as)


def heavy_noise(rng, dims, width, bound, cuts, heavy, kind=jnp.bfloat16):
    values = width * jax.random.normal(rng, dims, jnp.float32)
    if cuts:
        values = values * level_of(rng, dims, cuts, -0.22, 0.18)
    return jnp.clip(strengthened(values, jax.random.fold_in(rng, 3), *heavy), -bound, bound).astype(kind)


def setup_inputs(seed: int = 0) -> dict:
    splits = jax.random.split(jax.random.key(seed), 6)
    return {
        "velocities": gaussian(splits[0], (FBLK, N_ATOM * DOM_ROWS, 3 * FB_LEN), 1.0, 6.0, ((1, 16),)),
        "flux": gaussian(splits[1], (FBLK, N_ATOM * DOM_ROWS, 3 * FB_LEN), 1.0, 6.0, ((1, 16),)),
        "atom_ids": draw_atom_ids(jax.random.fold_in(splits[5], 71), 0),
        "row_counts": draw_row_counts(jax.random.fold_in(splits[5], 71), 0),
        "vectors": heavy_noise(splits[4], (3, ATOMS, MODES), (3 * ATOMS) ** -0.5, 0.0390625, ((1, 16), (2, 2)), (1, 2, 16, 2.0)),
    }


def reference(velocities, flux, atom_ids, row_counts, vectors):
    row_index = jnp.arange(DOM_ROWS, dtype=jnp.int32)
    signals = jnp.concatenate([velocities, flux], axis=2)
    owned_list = []
    for frame_block in range(FBLK):
        live_rows = (row_index[None, :] < row_counts[frame_block][:, None]).reshape(-1)
        target = jnp.where(live_rows, atom_ids[frame_block], ATOMS).astype(jnp.int32)
        owned_rows = jnp.zeros((ATOMS, 6 * FB_LEN), jnp.bfloat16).at[target].set(signals[frame_block], mode="drop")
        owned_list.append(owned_rows.reshape(ATOMS, 2, 3, FB_LEN))
    owned_all = jnp.stack(owned_list).astype(jnp.float32)

    def project(group_index):
        band_block = lax.dynamic_slice_in_dim(vectors, group_index * MODE_DEV, MODE_DEV, 2).astype(jnp.float32)
        return jnp.einsum("faqbt,ban->qftn", owned_all, band_block)

    projected = lax.map(project, jnp.arange(MODES // MODE_DEV, dtype=jnp.int32))
    projected = jnp.transpose(projected, (1, 2, 3, 0, 4)).reshape(2, FRAMES, MODES)
    heat_series = (projected[0] * projected[1]).astype(jnp.bfloat16)
    lead_rows = heat_series[:ANCHORS].T

    def lagged(lag_index):
        later_rows = lax.dynamic_slice_in_dim(heat_series, lag_index, ANCHORS, 0)
        product = jnp.dot(lead_rows, later_rows, preferred_element_type=jnp.float32)
        return (product * (1.0 / ANCHORS)).astype(jnp.bfloat16)

    return lax.map(lagged, jnp.arange(LAGS, dtype=jnp.int32))
```

```python
import functools

import jax
import jax.numpy as jnp
from jax import lax
from jax.experimental import pallas as pl
from jax.experimental.pallas import tpu as pltpu
from jax.sharding import PartitionSpec as P

LAGS = 16
F32 = jnp.float32
BF16 = jnp.bfloat16


def up(value, multiple):
    return -(-value // multiple) * multiple


def swap(x, axis, offset):
    names = axis if isinstance(axis, tuple) else (axis,)
    size = 1
    for name in names:
        size *= lax.axis_size(name)
    return lax.ppermute(x, axis, [(i, i ^ offset) for i in range(size)])


def iota(shape, dim):
    return lax.broadcasted_iota(jnp.int32, shape, dim)


def dot_nt(a, b):
    return lax.dot_general(a, b, (((1,), (1,)), ((), ())), preferred_element_type=F32)


def pack_kernel(lo, n_far, cap, rows_of, shift, sel_ref, me_ref, cnt_ref, ids_ref, vel_ref, flux_ref, a_ref, b_ref):
    block = sel_ref[pl.program_id(0)]
    ids = ids_ref[0]
    rows = ids.shape[1]
    buckets = 2 * n_far
    live = iota((1, rows), 1) < cnt_ref[block]
    key = lax.shift_right_logical(ids, shift) ^ me_ref[0]
    key = jnp.where(live, key - lo, -1)
    local = ids & ((1 << shift) - 1)
    hits = iota((buckets, rows), 0) == key
    hits_f = jnp.where(hits, 1.0, 0.0).astype(F32)
    before = jnp.where(iota((rows, rows), 0) < iota((rows, rows), 1), 1.0, 0.0).astype(BF16)
    earlier = jnp.dot(hits_f.astype(BF16), before, preferred_element_type=F32)
    rank = jnp.sum(hits_f * earlier, axis=0, keepdims=True).astype(jnp.int32)
    inside = (key >= 0) & (key < buckets)
    slot = (key & 1) * (n_far * rows_of) + lax.shift_right_logical(key, 1) * rows_of + rank
    slot = jnp.where(inside, slot, -1)
    place = jnp.where(iota((buckets * rows_of, rows), 0) == slot, 1.0, 0.0).astype(BF16)
    index_lanes = up(cap, 128)
    high = lax.shift_right_logical(local, 8).astype(F32)
    low = (local & 255).astype(F32)
    names = jnp.concatenate([hits_f * high, hits_f * low], axis=0).astype(BF16)
    at_rank = jnp.where(iota((index_lanes, rows), 0) == rank, 1.0, 0.0).astype(BF16)
    table = dot_nt(names, at_rank).astype(BF16)
    row = iota((buckets * rows_of, 2 * buckets), 0)
    col = iota((buckets * rows_of, 2 * buckets), 1)
    bucket = jnp.where(col < buckets, col, col - buckets)
    first = (bucket & 1) * (n_far * rows_of) + lax.shift_right_logical(bucket, 1) * rows_of
    spot = first + cap + jnp.where(col < buckets, 0, 1)
    spread = jnp.where(row == spot, 1.0, 0.0).astype(BF16)
    extra = jnp.dot(spread, table, preferred_element_type=F32)
    half = n_far * rows_of
    width = vel_ref.shape[2]
    for ref, start in ((vel_ref, 0), (flux_ref, width)):
        out = jnp.dot(place, ref[0], preferred_element_type=F32)
        if start == 0:
            out = jnp.concatenate([out[:, :index_lanes] + extra, out[:, index_lanes:]], axis=1)
        out = out.astype(BF16)
        a_ref[0, :, start : start + width] = out[:half]
        b_ref[0, :, start : start + width] = out[half:]


def pack(select, me, counts, ids, velocities, flux, lo, n_far, cap, rows_of, shift):
    steps = select.shape[0]
    rows, width = velocities.shape[1:]
    half = n_far * rows_of

    def pick(i, sel, *_):
        return (sel[i], 0, 0)

    def own(i, *_):
        return (i, 0, 0)

    return pl.pallas_call(
        functools.partial(pack_kernel, lo, n_far, cap, rows_of, shift),
        out_shape=[jax.ShapeDtypeStruct((steps, half, 2 * width), BF16)] * 2,
        grid_spec=pltpu.PrefetchScalarGridSpec(
            num_scalar_prefetch=3,
            grid=(steps,),
            in_specs=[
                pl.BlockSpec((1, 1, rows), pick),
                pl.BlockSpec((1, rows, width), pick),
                pl.BlockSpec((1, rows, width), pick),
            ],
            out_specs=[pl.BlockSpec((1, half, 2 * width), own)] * 2,
        ),
        cost_estimate=pl.CostEstimate(
            flops=4 * steps * half * rows * 2 * width,
            bytes_accessed=8 * steps * rows * width,
            transcendentals=0,
        ),
        name="pack",
    )(select, me, counts, ids, velocities, flux)


def bucket_matches(index_ref_row, cap, n_rows, first_atom):
    lanes = index_ref_row.shape[1]
    held = iota((1, lanes), 1) < cap
    target = jnp.where(held, index_ref_row, -1)
    return jnp.where(iota((n_rows, lanes), 0) + first_atom == target, 1.0, 0.0).astype(BF16)


def unpack_kernel(cap, rows_of, n_parts, has_base, project, *refs):
    refs = list(refs)
    if has_base or project:
        refs.pop(0)
    parts = refs[:n_parts]
    refs = refs[n_parts:]
    base = refs.pop(0) if has_base else None
    basis = refs.pop(0) if project else None
    if project and len(refs) == 5:
        refs.pop(0)
    out_ref, stage, names = refs[:3]
    acc = refs[3] if project else None
    step = pl.program_id(0)
    lanes = up(cap, 128)
    n_buckets = sum(p.shape[-2] // rows_of for p in parts)
    width = stage.shape[1]

    @pl.when(step == 0)
    def _():
        spot = 0
        for p in parts:
            for j in range(p.shape[-2] // rows_of):
                data = p[0, j * rows_of : (j + 1) * rows_of, :]
                stage[spot * lanes : spot * lanes + rows_of, :] = data
                stage[spot * lanes + rows_of : (spot + 1) * lanes, :] = jnp.zeros((lanes - rows_of, width), BF16)
                high = data[cap : cap + 1, :lanes].astype(F32)
                low = data[cap + 1 : cap + 2, :lanes].astype(F32)
                value = high * 256.0 + low
                value = jnp.where(iota((1, lanes), 1) < cap, value, -1.0)
                names[0:1, spot * lanes : (spot + 1) * lanes] = value.astype(jnp.int32)
                spot += 1
        if acc is not None:
            acc[...] = jnp.zeros_like(acc)

    atoms = out_ref.shape[1] if not project else basis.shape[2]
    target = names[0:1, :]
    match = jnp.where(iota((atoms, n_buckets * lanes), 0) + step * atoms == target, 1.0, 0.0).astype(BF16)
    owned = jnp.dot(match, stage[...], preferred_element_type=F32)
    if base is not None:
        owned = owned + base[0].astype(F32)
    owned = owned.astype(BF16)
    if not project:
        out_ref[0] = owned
        return
    frames = width // 6
    total = acc[...]
    for b in range(3):
        cols = jnp.concatenate(
            [owned[:, b * frames : (b + 1) * frames], owned[:, (3 + b) * frames : (4 + b) * frames]], axis=1
        )
        total = total + jnp.dot(basis[b], cols, preferred_element_type=F32)
    acc[...] = total

    @pl.when(step == pl.num_programs(0) - 1)
    def _():
        out_ref[...] = acc[...].astype(BF16)


def gather_near(parts, cap, rows_of, owned_count):
    width = parts[0].shape[2]
    blocks = parts[0].shape[0]
    n_buckets = sum(p.shape[1] // rows_of for p in parts)
    lanes = up(cap, 128)

    def kernel(*refs):
        ins, out_ref, stage, names = refs[: len(parts)], refs[-3], refs[-2], refs[-1]
        spot = 0
        for p in ins:
            for j in range(p.shape[1] // rows_of):
                data = p[0, j * rows_of : (j + 1) * rows_of, :]
                stage[spot * lanes : spot * lanes + rows_of, :] = data
                stage[spot * lanes + rows_of : (spot + 1) * lanes, :] = jnp.zeros((lanes - rows_of, width), BF16)
                high = data[cap : cap + 1, :lanes].astype(F32)
                low = data[cap + 1 : cap + 2, :lanes].astype(F32)
                value = jnp.where(iota((1, lanes), 1) < cap, high * 256.0 + low, -1.0)
                names[0:1, spot * lanes : (spot + 1) * lanes] = value.astype(jnp.int32)
                spot += 1
        match = jnp.where(iota((owned_count, n_buckets * lanes), 0) == names[0:1, :], 1.0, 0.0).astype(BF16)
        out_ref[0] = jnp.dot(match, stage[...], preferred_element_type=F32).astype(BF16)

    return pl.pallas_call(
        kernel,
        out_shape=jax.ShapeDtypeStruct((blocks, owned_count, width), BF16),
        grid=(blocks,),
        in_specs=[pl.BlockSpec((1,) + p.shape[1:], lambda i: (i, 0, 0)) for p in parts],
        out_specs=pl.BlockSpec((1, owned_count, width), lambda i: (i, 0, 0)),
        scratch_shapes=[
            pltpu.VMEM((n_buckets * lanes, width), BF16),
            pltpu.VMEM((8, n_buckets * lanes), jnp.int32),
        ],
        cost_estimate=pl.CostEstimate(
            flops=4 * owned_count * n_buckets * lanes * width, bytes_accessed=8 * owned_count * width, transcendentals=0
        ),
        name="near",
    )(*parts)


def project_far(select, parts, base, basis, whole, half_index, cap, rows_of):
    width = parts[0].shape[2]
    n_buckets = sum(p.shape[1] // rows_of for p in parts)
    lanes = up(cap, 128)
    owned_count = base.shape[1]
    modes = basis.shape[1]
    steps = 4
    chunk = owned_count // steps
    frames = width // 6
    in_specs = [pl.BlockSpec(p.shape, lambda i, s: (0, 0, 0)) for p in parts]
    in_specs.append(pl.BlockSpec((1, chunk, width), lambda i, s: (s[0], i, 0)))
    in_specs.append(pl.BlockSpec((3, modes, chunk), lambda i, s: (0, 0, i)))
    operands = list(parts) + [base, basis]
    aliases = {}
    if whole is not None:
        in_specs.append(pl.BlockSpec(memory_space=pl.ANY))
        aliases = {1 + len(operands): 0}
        operands.append(whole)
    return pl.pallas_call(
        functools.partial(unpack_kernel, cap, rows_of, len(parts), True, True),
        out_shape=jax.ShapeDtypeStruct((modes, 4 * frames), BF16),
        grid_spec=pltpu.PrefetchScalarGridSpec(
            num_scalar_prefetch=1,
            grid=(steps,),
            in_specs=in_specs,
            out_specs=pl.BlockSpec((modes, 2 * frames), lambda i, s: (0, half_index)),
            scratch_shapes=[
                pltpu.VMEM((n_buckets * lanes, width), BF16),
                pltpu.VMEM((8, n_buckets * lanes), jnp.int32),
                pltpu.VMEM((modes, 2 * frames), F32),
            ],
        ),
        input_output_aliases=aliases,
        cost_estimate=pl.CostEstimate(
            flops=2 * owned_count * width * (n_buckets * lanes + modes),
            bytes_accessed=2 * owned_count * (width + 3 * modes),
            transcendentals=0,
        ),
        name="project",
    )(select, *operands)


def heat_kernel(sel_ref, pieces_ref, out_ref):
    total = jnp.sum(pieces_ref[...].astype(F32), axis=0)
    frames = total.shape[1] // 4
    mine = total[:, :frames] * total[:, frames : 2 * frames]
    other = total[:, 2 * frames : 3 * frames] * total[:, 3 * frames :]
    swapped = sel_ref[0] != 0
    out_ref[:, :frames] = jnp.where(swapped, other, mine).astype(BF16)
    out_ref[:, frames:] = jnp.where(swapped, mine, other).astype(BF16)


def heat_of(select, pieces):
    n, rows, lanes = pieces.shape
    return pl.pallas_call(
        heat_kernel,
        out_shape=jax.ShapeDtypeStruct((rows, lanes // 2), BF16),
        grid_spec=pltpu.PrefetchScalarGridSpec(
            num_scalar_prefetch=1,
            grid=(1,),
            in_specs=[pl.BlockSpec((n, rows, lanes), lambda i, s: (0, 0, 0))],
            out_specs=pl.BlockSpec((rows, lanes // 2), lambda i, s: (0, 0)),
        ),
        name="heat",
    )(select, pieces)


def lag_kernel(order, width, anchors, me_ref, own_ref, a_ref, b_ref, out_ref, series):
    frames = own_ref.shape[1]
    for i, offset in enumerate(order):
        for ref, extra in ((a_ref, 0), (b_ref, 1)):
            start = pl.multiple_of((me_ref[0] ^ (offset ^ extra)) * width, width)
            series[pl.ds(start, width), :] = ref[i * width : (i + 1) * width, :]
    lead = jnp.where(iota((width, frames), 1) < anchors, own_ref[...].astype(F32), 0.0)
    lagged = [lead if k == 0 else pltpu.roll(lead, k, 1) for k in range(LAGS)]
    lagged = jnp.concatenate(lagged, axis=0).astype(BF16)
    out = dot_nt(lagged, series[...]) * (1.0 / anchors)
    for k in range(LAGS):
        out_ref[k] = out[k * width : (k + 1) * width].astype(BF16)


def lags_of(me, own, a, b, order, modes, anchors):
    width, frames = own.shape
    return pl.pallas_call(
        functools.partial(lag_kernel, order, width, anchors),
        out_shape=jax.ShapeDtypeStruct((LAGS, width, modes), BF16),
        grid_spec=pltpu.PrefetchScalarGridSpec(
            num_scalar_prefetch=1,
            grid=(1,),
            in_specs=[
                pl.BlockSpec(own.shape, lambda i, s: (0, 0)),
                pl.BlockSpec(a.shape, lambda i, s: (0, 0)),
                pl.BlockSpec(b.shape, lambda i, s: (0, 0)),
            ],
            out_specs=pl.BlockSpec((LAGS, width, modes), lambda i, s: (0, 0, 0)),
            scratch_shapes=[pltpu.VMEM((modes, frames), BF16)],
        ),
        name="lags",
    )(me, own, a, b)


def xor_offsets(bits):
    offsets = [0]
    for bit in bits:
        offsets = offsets + [o | bit for o in offsets]
    return offsets


def body(velocities, flux, atom_ids, row_counts, vectors):
    domains, bands = lax.axis_size("atom"), lax.axis_size("mode")
    blocks, dom_rows, _ = velocities.shape
    owned_count, band_width = vectors.shape[1:]
    shift = owned_count.bit_length() - 1
    cap = dom_rows // domains
    rows_of = up(cap + 2, 8)
    chips = domains // 2
    near = chips // 2
    me = lax.axis_index("atom").astype(jnp.int32)
    band = lax.axis_index("mode").astype(jnp.int32)
    mine = jnp.reshape(band & 1, (1,))
    other = 1 - mine
    me1 = jnp.reshape(me, (1,))
    counts = row_counts.reshape(blocks)
    ids = atom_ids.reshape(blocks, 1, dom_rows)
    settings = (cap, rows_of, shift)

    far_a, far_b = pack(mine, me1, counts, ids, velocities, flux, 2 * near, chips - near, *settings)
    far_b = swap(far_b, "atom", 1)
    far = []
    for i in range(chips - near):
        part = slice(i * rows_of, (i + 1) * rows_of)
        bundle = jnp.concatenate([far_a[:, part], far_b[:, part]], axis=1)
        far.append(swap(bundle, "atom", 2 * (near + i)))
    both = jnp.arange(blocks, dtype=jnp.int32)
    near_a, near_b = pack(both, me1, counts, ids, velocities, flux, 0, near, *settings)
    near_b = swap(near_b, "atom", 1)
    parts = [near_a[:, :rows_of], near_b[:, :rows_of]]
    for i in range(1, near):
        part = slice(i * rows_of, (i + 1) * rows_of)
        bundle = jnp.concatenate([near_a[:, part], near_b[:, part]], axis=1)
        parts.append(swap(bundle, "atom", 2 * i))
    passed = [swap(x, "mode", 1) for x in far]

    basis = jnp.swapaxes(vectors, 1, 2)
    base = gather_near(parts, cap, rows_of, owned_count)
    partial_value = project_far(mine, far, base, basis, None, 0, cap, rows_of)
    partial_value = project_far(other, passed, base, basis, partial_value, 1, cap, rows_of)

    frames = partial_value.shape[1] // 2
    own_width = band_width // domains
    pieces = partial_value.reshape(domains, own_width, 2 * frames)
    pieces = lax.all_to_all(pieces, "atom", split_axis=0, concat_axis=0, tiled=True)
    heat = heat_of(mine, pieces)

    everyone = ("mode", "atom")
    mode_bits = [domains << i for i in range(bands.bit_length() - 1)]
    atom_bits = [1 << i for i in range(domains.bit_length() - 1)]
    series, order = heat, [0]
    for bits in (mode_bits + atom_bits[1:2], atom_bits[2:]):
        offsets = xor_offsets(bits)
        series = jnp.concatenate([series if o == 0 else swap(series, everyone, o) for o in offsets], axis=0)
        order = [o ^ p for o in offsets for p in order]
    sibling = swap(series, everyone, 1)
    return lags_of(
        jnp.reshape(band * domains + me, (1,)),
        heat,
        series,
        sibling,
        order,
        bands * band_width,
        frames - LAGS + 1,
    )


def solution(mesh):
    in_specs = (
        P(None, "atom", None),
        P(None, "atom", None),
        P(None, "atom"),
        P(None, "atom"),
        P(None, "atom", "mode"),
    )
    out_specs = P(None, ("mode", "atom"), None)
    return jax.shard_map(body, mesh=mesh, in_specs=in_specs, out_specs=out_specs, check_vma=False)
```
